32 devices in a mesh: map: 2 (over x), rows: 16 (over z, y, core).
Axes of the slice: x: 2, y: 2, z: 4, core: 2. Of those that a mesh axis runs over, the one named last changes fastest.
Arguments:
- density: bfloat16 [16, 2048, 2048], P('map', 'rows'), parts along dimension 0, may hold values from 0 to 2300, as said below
- lens_weight: float32 [8], replicated, may hold values from 0.05 to 0.5
- bin_distance: float32 [16], replicated, may hold values from 0.5 to 2.5, as said below
- plane_bin: int32 [8], replicated, may hold values from 0 to 15, as said below
- source_plane: int32 [1], replicated, may hold values from 1 to 7, as said below
Outputs:
- shear: float32 [2, 2, 2048, 2048], P('map', None, 'rows'), parts along dimension 0
The draws below stay inside these ranges and needn't reach their ends.
There are 2 independent parts, one for each index of `map`. The reference program is written for one: setup_inputs(seed, part) draws one part's arguments, and reference() takes and returns one part's arrays. A program takes and returns all parts, laid end to end along the dimension named above; an argument that names none is the same for every part. Nothing has to cross between parts.
Inputs may be any that keep to these rules, and one draw needn't show every extreme that they name: `density`: positive. `bin_distance`: increasing. `plane_bin`: strictly increasing over the planes. `source_plane`: distinct and increasing.
All inputs are finite; a program needn't handle non-finite values.
Results may differ from the reference program's by a relative error of at most 0.0003.
Values sent between devices are 32-bit elements; how exact they have to be, the bound alone decides.
No kernel may reach another device: no remote copies, remote signals or barrier semaphores. Data moves between devices by JAX's collectives and lax.ppermute only.
A program may use at most 64 MiB of HBM per device.

```python
import math
import jax
import jax.numpy as jnp
from jax import lax

NX = 2048
NY = 2048
PLANES = 8
SOURCES = 1
NBINS = 16


def draw_density(key, part):
    key_rows, key_cols, key_planes, key_base = jax.random.split(key, 4)
    rows_frac = jnp.arange(NX, dtype=jnp.float32) / NX
    row_power = 0.5 * rows_frac + 0.5 * jax.random.uniform(key_rows, (NX,), dtype=jnp.float32)
    col_power = jax.random.uniform(key_cols, (NY,), dtype=jnp.float32)
    plane_power = jax.random.uniform(key_planes, (PLANES,), dtype=jnp.float32, minval=-0.3, maxval=0.3)
    normals = jnp.clip(jax.random.normal(key_base, (PLANES, NX, NY), dtype=jnp.float32), -4.0, 4.0)
    base = jnp.exp(0.6 * normals)
    power = row_power[None, :, None] + col_power[None, None, :] + plane_power[:, None, None]
    return (base * jnp.power(10.0, power)).astype(jnp.bfloat16)


def draw_bin_distance(key, part):
    steps_drawn = jax.random.uniform(key, (NBINS,), dtype=jnp.float32, minval=0.5, maxval=1.5)
    running = jnp.cumsum(steps_drawn) - steps_drawn[0]
    return 0.5 + 2.0 * running / running[NBINS - 1]


def draw_plane_bin(key, part):
    inner = jax.random.permutation(key, NBINS - 2)[:PLANES - 2].astype(jnp.int32) + 1
    chosen = jnp.concatenate([jnp.zeros((1,), jnp.int32), inner, jnp.full((1,), NBINS - 1, jnp.int32)])
    return jnp.sort(chosen)


def draw_source_plane(key, part):
    inner = jax.random.permutation(key, PLANES - 2)[:SOURCES - 1].astype(jnp.int32) + 1
    chosen = jnp.concatenate([inner, jnp.full((1,), PLANES - 1, jnp.int32)])
    return jnp.sort(chosen)


def setup_inputs(seed: int = 0, part: int = 0) -> dict:
    key_of = jax.random.split(jax.random.key(seed), 6)
    part_splits = jax.random.split(jax.random.fold_in(key_of[5], part), 6)
    density = draw_density(jax.random.fold_in(jax.random.fold_in(key_of[5], part), 71), part)
    lens_weight = jnp.clip(jnp.exp(jax.random.uniform(key_of[1], (PLANES,), jnp.float32, math.log(0.05), math.log(0.5))), 0.05, 0.5)
    bin_distance = draw_bin_distance(jax.random.fold_in(key_of[5], 71), part)
    plane_bin = draw_plane_bin(jax.random.fold_in(key_of[5], 71), part)
    source_plane = draw_source_plane(jax.random.fold_in(key_of[5], 71), part)
    return {"density": density, "lens_weight": lens_weight, "bin_distance": bin_distance, "plane_bin": plane_bin, "source_plane": source_plane}


def signed_frequency(positions, length):
    return jnp.where(positions < length // 2, positions, positions - length).astype(jnp.float32) / length


def shear_kernel(row_positions, col_positions, total_rows, total_cols):
    wave_rows = signed_frequency(row_positions, total_rows)[:, None]
    wave_cols = signed_frequency(col_positions, total_cols)[None, :]
    squared = wave_rows * wave_rows + wave_cols * wave_cols
    denominator = jnp.where(squared > 0, squared, jnp.float32(1.0))
    return (wave_rows * wave_rows - wave_cols * wave_cols) / denominator, 2.0 * wave_rows * wave_cols / denominator


def lens_coefficients(lens_weight, bin_distance, plane_bin, source_plane):
    bin_ids = jnp.arange(bin_distance.shape[0], dtype=jnp.int32)
    distance = jnp.sum(jnp.where(plane_bin[:, None] == bin_ids[None, :], bin_distance[None, :], jnp.float32(0.0)), axis=1)
    planes = jnp.arange(plane_bin.shape[0], dtype=jnp.int32)
    picked = source_plane[:, None] == planes[None, :]
    source_distance = jnp.sum(jnp.where(picked, distance[None, :], jnp.float32(0.0)), axis=1)
    nearer = planes[None, :] <= source_plane[:, None]
    weights = lens_weight[None, :] * (1.0 - distance[None, :] / source_distance[:, None])
    return jnp.where(nearer, weights, jnp.float32(0.0))


def reference(density, lens_weight, bin_distance, plane_bin, source_plane):
    total_rows = density.shape[1]
    total_cols = density.shape[2]
    plane_mean = jnp.sum(density.astype(jnp.float32), axis=(1, 2)) / (total_rows * total_cols)
    contrast = density.astype(jnp.float32) / plane_mean[:, None, None] - 1.0
    coefficients = lens_coefficients(lens_weight, bin_distance, plane_bin, source_plane)
    convergence = jnp.einsum('sl,lxy->sxy', coefficients, contrast, precision=lax.Precision.HIGHEST)
    spectrum = jnp.fft.fft2(convergence, axes=(1, 2))
    kernel_plus, kernel_cross = shear_kernel(jnp.arange(total_rows, dtype=jnp.int32), jnp.arange(total_cols, dtype=jnp.int32), total_rows, total_cols)
    sheared = lax.complex(kernel_plus, kernel_cross)[None] * spectrum
    returned = jnp.fft.ifft2(sheared, axes=(1, 2))
    return jnp.stack([jnp.real(returned), jnp.imag(returned)], axis=1)
```

```python
import functools

import jax
import jax.numpy as jnp
import numpy as np
from jax import lax
from jax.experimental import pallas as pl
from jax.experimental.pallas import tpu as pltpu
from jax.sharding import PartitionSpec as P

LANES = 128
HIGHEST = lax.Precision.HIGHEST


def signed_frequency(positions, length):
    return (
        jnp.where(positions < length // 2, positions, positions - length).astype(jnp.float32)
        / length
    )


def kernel_terms(row_freq, col_freq, total_rows, total_cols):
    wave_rows = signed_frequency(row_freq, total_rows)
    wave_cols = signed_frequency(col_freq, total_cols)
    squared = wave_rows * wave_rows + wave_cols * wave_cols
    denominator = jnp.where(squared > 0, squared, jnp.float32(1.0))
    return (
        (wave_rows * wave_rows - wave_cols * wave_cols) / denominator,
        2.0 * wave_rows * wave_cols / denominator,
    )


def lens_coefficients(lens_weight, bin_distance, plane_bin, source_plane):
    bin_ids = jnp.arange(bin_distance.shape[0], dtype=jnp.int32)
    distance = jnp.sum(
        jnp.where(plane_bin[:, None] == bin_ids[None, :], bin_distance[None, :], jnp.float32(0.0)),
        axis=1,
    )
    planes = jnp.arange(plane_bin.shape[0], dtype=jnp.int32)
    picked = source_plane[:, None] == planes[None, :]
    source_distance = jnp.sum(jnp.where(picked, distance[None, :], jnp.float32(0.0)), axis=1)
    nearer = planes[None, :] <= source_plane[:, None]
    weights = lens_weight[None, :] * (1.0 - distance[None, :] / source_distance[:, None])
    return jnp.where(nearer, weights, jnp.float32(0.0))


def rotate(value, turns, orient):
    re, im = value
    turns = turns % 1.0
    if turns == 0.0:
        return re, im
    cos, sin = float(np.cos(2 * np.pi * turns)), float(orient * np.sin(2 * np.pi * turns))
    if turns == 0.25:
        return (None if im is None else -im * sin if sin != 1.0 else -im), (re if sin > 0 else -re)
    if im is None:
        return re * cos, re * sin
    return re * cos - im * sin, re * sin + im * cos


def plus(a, b):
    return b if a is None else a if b is None else a + b


def minus(a, b):
    return (None if b is None else -b) if a is None else a if b is None else a - b


def real_fft(values):
    n = len(values)
    if n == 1:
        return [(values[0], None)]
    if n == 2:
        return [(values[0] + values[1], None), (values[0] - values[1], None)]
    even, odd = real_fft(values[0::2]), real_fft(values[1::2])
    half, quarter = n // 2, n // 4
    out = [None] * (half + 1)
    for k in range(quarter + 1):
        e, o = even[k], rotate(odd[k], k / n, -1.0)
        out[k] = plus(e[0], o[0]), plus(e[1], o[1])
        if k != half - k:
            diff = minus(e[0], o[0]), minus(e[1], o[1])
            out[half - k] = diff[0], None if diff[1] is None else -diff[1]
    out[0], out[half] = (out[0][0], None), (out[half][0], None)
    return out


def real_inverse(values):
    half = len(values) - 1
    n = 2 * half
    if n == 2:
        return [values[0][0] + values[1][0], values[0][0] - values[1][0]]
    even, odd = [], []
    for k in range(half // 2 + 1):
        a, b = values[k], values[half - k]
        conj_im = None if b[1] is None else -b[1]
        if k == half - k:
            even.append((2.0 * a[0], None))
            odd.append((-2.0 * a[1], None))
            continue
        even.append((a[0] + b[0], plus(a[1], conj_im)))
        odd.append(rotate((a[0] - b[0], minus(a[1], conj_im)), k / n, 1.0))
    even[0], odd[0] = (even[0][0], None), (odd[0][0], None)
    out = [None] * n
    out[0::2], out[1::2] = real_inverse(even), real_inverse(odd)
    return out


def packed_fft(values, orient, turn):
    n = len(values)
    if n == 1:
        return values
    even, odd = packed_fft(values[0::2], orient, turn), packed_fft(values[1::2], orient, turn)
    out = [None] * n
    for k in range(n // 2):
        o = odd[k]
        if 4 * k == n:
            t = turn(o)
            lo, hi = (t, True) if orient < 0 else (t, False)
            out[k] = even[k] + lo if hi else even[k] - lo
            out[k + n // 2] = even[k] - lo if hi else even[k] + lo
            continue
        if k:
            cos = float(np.cos(2 * np.pi * k / n))
            sin = float(-orient * np.sin(2 * np.pi * k / n))
            o = o * cos + turn(o) * sin
        out[k], out[k + n // 2] = even[k] + o, even[k] - o
    return out


def column_frequencies(positions, total_cols):
    groups = total_cols // LANES
    block, q = positions // LANES, positions % LANES
    first = jnp.where(q < LANES // 2, groups * q, groups // 2 + groups * (q - LANES // 2))
    ky = jnp.where(block == 0, first, block + groups * q)
    return jnp.where(positions == 0, total_cols // 2, ky)


def col_tables(share, total):
    b = np.arange(LANES)[:, None]
    q = np.arange(LANES)[None, :]
    re_lane = (q // share * 2 * share + q % share)[0]
    im_lane = re_lane + share
    ang = 2 * np.pi * (b * q % LANES) / LANES
    fwd = np.zeros((2 * LANES, 2 * LANES))
    fwd[:LANES, re_lane], fwd[:LANES, im_lane] = np.cos(ang), -np.sin(ang)
    fwd[LANES:, re_lane], fwd[LANES:, im_lane] = np.sin(ang), np.cos(ang)
    inv = fwd.T.copy()
    half = LANES // 2
    fwd0 = np.zeros((2 * LANES, 2 * LANES))
    inv0 = np.zeros((2 * LANES, 2 * LANES))
    ang0 = ang[:, :half]
    ang1 = 2 * np.pi * (b * (2 * q[:, :half] + 1) % (2 * LANES)) / (2 * LANES)
    fwd0[:LANES, re_lane[:half]], fwd0[:LANES, im_lane[:half]] = np.cos(ang0), -np.sin(ang0)
    fwd0[LANES:, re_lane[half:]], fwd0[LANES:, im_lane[half:]] = np.cos(ang1), -np.sin(ang1)
    fwd0[:LANES, re_lane[0]], fwd0[:LANES, im_lane[0]] = (-1.0) ** b[:, 0], 1.0
    inv0 = 2.0 * fwd0.T
    inv0[re_lane[0]] *= 0.5
    inv0[im_lane[0]] *= 0.5
    return fwd, fwd0, inv, inv0


def forward_rows(scale_ref, density_ref, fwd_ref, fwd0_ref, twist_ref, out_ref, held):
    planes, rows, total_cols = density_ref.shape
    groups = total_cols // LANES
    width = out_ref.shape[2]
    tile = min(16, rows)

    def step(t, carry):
        here = pl.ds(pl.multiple_of(t * tile, tile), tile)
        values = []
        for a in range(groups):
            total = density_ref[0, here, a * LANES:(a + 1) * LANES].astype(jnp.float32) * scale_ref[0] - scale_ref[planes]
            for l in range(1, planes):
                total += density_ref[l, here, a * LANES:(a + 1) * LANES].astype(jnp.float32) * scale_ref[l]
            values.append(total)
        spectrum = real_fft(values)
        held[0, here, :LANES] = spectrum[0][0]
        held[0, here, LANES:] = spectrum[groups // 2][0]
        for k in range(1, groups // 2):
            re, im = spectrum[k]
            cos, sin = twist_ref[0, k:k + 1, :], twist_ref[1, k:k + 1, :]
            held[k, here, :LANES] = re * cos + im * sin
            held[k, here, LANES:] = im * cos - re * sin
        return carry

    lax.fori_loop(0, rows // tile, step, 0)
    for k in range(groups // 2):
        matrix = fwd0_ref[...] if k == 0 else fwd_ref[...]
        product = jnp.dot(held[k], matrix, precision=HIGHEST, preferred_element_type=jnp.float32)
        per = 2 * LANES // width
        for g in range(per):
            out_ref[k * per + g] = product[:, g * width:(g + 1) * width]


def columns_step(flag_ref, in_ref, fwd_ref, inv_ref, even_ref, cross_ref, odd_ref, first_ref, second_ref, work, both):
    devices, rows, width = in_ref.shape
    share = width // 2
    total_rows = devices * rows
    lane = lax.broadcasted_iota(jnp.int32, (1, width), 1)
    special = jnp.where(lane == share, flag_ref[0], 0.0)
    keep = 1.0 - special
    sign = jnp.where(lane < share, 1.0, -1.0)

    def turn(v):
        if width == LANES:
            return pltpu.roll(v, share, 1) * sign
        return jnp.concatenate([v[:, share:], -v[:, :share]], axis=1)

    tile = 8

    def forward(t, total):
        here = pl.ds(pl.multiple_of(t * tile, tile), tile)
        values = [in_ref[a, here, :] for a in range(devices)]
        total = total + functools.reduce(lambda x, y: x + y, values)
        out = packed_fft([v * keep for v in values], -1.0, turn)
        for k in range(devices):
            work[k, here, :] = out[k]
            work[k, pl.ds(pl.multiple_of(rows + t * tile, tile), tile), :] = turn(out[k])
        return total

    total = lax.fori_loop(0, rows // tile, forward, jnp.zeros((tile, width), jnp.float32))
    mean = jnp.sum(total, axis=0, keepdims=True) / total_rows
    for k in range(devices):
        spectrum = jnp.dot(fwd_ref[k], work[k], precision=HIGHEST, preferred_element_type=jnp.float32)
        turned = turn(spectrum)
        even, cross, odd = even_ref[k], cross_ref[k], odd_ref[k]
        sheared = jnp.concatenate(
            [
                jnp.concatenate([even * spectrum - odd * turned, cross * spectrum], axis=1),
                jnp.concatenate([even * turned + odd * spectrum, cross * turned], axis=1),
            ],
            axis=0,
        )
        both[k] = jnp.dot(inv_ref[k], sheared, precision=HIGHEST, preferred_element_type=jnp.float32)

    def backward(t, carry):
        here = pl.ds(pl.multiple_of(t * tile, tile), tile)
        for out_ref, start in ((first_ref, 0), (second_ref, width)):
            out = packed_fft([both[k, here, start:start + width] for k in range(devices)], 1.0, turn)
            for a in range(devices):
                value = out[a]
                if start == 0:
                    value = value + (in_ref[a, here, :] - mean) * (special * float(total_rows))
                out_ref[a, here, :] = value
        return carry

    lax.fori_loop(0, rows // tile, backward, 0)


def inverse_rows(first_ref, second_ref, inv_ref, inv0_ref, twist_ref, out_ref, held):
    devices, rows, width = first_ref.shape
    total_cols = out_ref.shape[3]
    groups = total_cols // LANES
    per = 2 * LANES // width
    tile = 8
    for f, ref in enumerate((first_ref, second_ref)):
        for k in range(groups // 2):
            matrix = inv0_ref[...] if k == 0 else inv_ref[...]
            value = jnp.concatenate([ref[k * per + g] for g in range(per)], axis=1)
            held[f, k] = jnp.dot(value, matrix, precision=HIGHEST, preferred_element_type=jnp.float32)

        def step(t, carry):
            here = pl.ds(pl.multiple_of(t * tile, tile), tile)
            values = [(held[f, 0, here, :LANES], None)]
            for k in range(1, groups // 2):
                re, im = held[f, k, here, :LANES], held[f, k, here, LANES:]
                cos, sin = twist_ref[0, k:k + 1, :], twist_ref[1, k:k + 1, :]
                values.append((re * cos - im * sin, re * sin + im * cos))
            values.append((held[f, 0, here, LANES:], None))
            out = real_inverse(values)
            for a in range(groups):
                out_ref[0, f, here, a * LANES:(a + 1) * LANES] = out[a]
            return carry

        lax.fori_loop(0, rows // tile, step, 0)


def smem():
    return pl.BlockSpec(memory_space=pltpu.SMEM)


def vmem():
    return pl.BlockSpec(memory_space=pltpu.VMEM)


def phase_tables(devices, rows):
    total = devices * rows
    k, j = np.arange(devices), np.arange(rows)
    turns = 2 * np.pi * np.outer(k, j) / total
    inner = 2 * np.pi * (np.outer(j, j) % rows) / rows
    tc, ts = jnp.asarray(np.cos(turns), jnp.float32), jnp.asarray(np.sin(turns), jnp.float32)
    ic, is_ = jnp.asarray(np.cos(inner), jnp.float32), jnp.asarray(np.sin(inner), jnp.float32)
    cos = tc[:, None, :] * ic - ts[:, None, :] * is_
    sin = ts[:, None, :] * ic + tc[:, None, :] * is_
    fwd = jnp.concatenate([cos, sin], axis=2)
    cos_t = tc[:, :, None] * ic - ts[:, :, None] * is_
    sin_t = ts[:, :, None] * ic + tc[:, :, None] * is_
    return fwd, jnp.concatenate([cos_t, -sin_t], axis=2)


def on_device(density, lens_weight, bin_distance, plane_bin, source_plane):
    planes, rows, total_cols = density.shape
    devices = lax.axis_size("rows")
    total_rows = rows * devices
    share = total_cols // 2 // devices
    width = 2 * share
    groups = total_cols // LANES

    plane_sums = jnp.sum(density, axis=(1, 2), dtype=jnp.float32)
    spread = jnp.broadcast_to(plane_sums[None, None, :], (devices, 1, planes))
    gathered = lax.all_to_all(spread, "rows", split_axis=0, concat_axis=0, tiled=True)
    plane_mean = jnp.sum(gathered, axis=(0, 1)) / (total_rows * total_cols)
    coefficients = lens_coefficients(lens_weight, bin_distance, plane_bin, source_plane)[0]
    scale = jnp.concatenate([coefficients / plane_mean, jnp.sum(coefficients)[None]])

    fwd, fwd0, inv, inv0 = col_tables(share, total_cols)
    norm = 1.0 / (total_rows * total_cols)
    as_f32 = lambda table: jnp.asarray(table, jnp.float32)
    angle = 2 * np.pi * np.outer(np.arange(groups // 2), np.arange(LANES)) / total_cols
    twist = as_f32(np.stack([np.cos(angle), np.sin(angle)]))

    send = pl.pallas_call(
        forward_rows,
        out_shape=jax.ShapeDtypeStruct((devices, rows, width), jnp.float32),
        in_specs=[smem()] + [vmem()] * 4,
        out_specs=vmem(),
        scratch_shapes=[pltpu.VMEM((groups // 2, rows, 2 * LANES), jnp.float32)],
        name="forward_rows",
    )(scale, density, as_f32(fwd), as_f32(fwd0), twist)
    columns = lax.all_to_all(send, "rows", split_axis=0, concat_axis=0, tiled=True)

    index = lax.axis_index("rows")
    row_freq = (
        jnp.arange(devices, dtype=jnp.int32)[:, None] + devices * jnp.arange(rows, dtype=jnp.int32)[None, :]
    )[:, :, None]
    lanes = jnp.arange(width, dtype=jnp.int32) % share
    col_freq = column_frequencies(index * share + lanes, total_cols)[None, None, :]
    even, cross = kernel_terms(row_freq, col_freq, total_rows, total_cols)
    is_odd = (row_freq == total_rows // 2) != (col_freq == total_cols // 2)
    odd = jnp.where(is_odd, cross, 0.0)
    cross = jnp.where(is_odd, 0.0, cross)
    col_fwd, col_inv = phase_tables(devices, rows)
    flag = (index == 0).astype(jnp.float32)[None]
    block = jax.ShapeDtypeStruct((devices, rows, width), jnp.float32)
    first, second = pl.pallas_call(
        columns_step,
        out_shape=(block, block),
        in_specs=[smem()] + [vmem()] * 6,
        out_specs=(vmem(), vmem()),
        scratch_shapes=[
            pltpu.VMEM((devices, 2 * rows, width), jnp.float32),
            pltpu.VMEM((devices, rows, 2 * width), jnp.float32),
        ],
        name="columns_step",
    )(flag, columns, col_fwd, col_inv, even, cross, odd)

    back = lax.all_to_all(
        jnp.stack([first, second], axis=1), "rows", split_axis=0, concat_axis=0, tiled=True
    )
    first, second = back[:, 0], back[:, 1]

    return pl.pallas_call(
        inverse_rows,
        out_shape=jax.ShapeDtypeStruct((1, 2, rows, total_cols), jnp.float32),
        in_specs=[vmem()] * 5,
        out_specs=vmem(),
        scratch_shapes=[pltpu.VMEM((2, groups // 2, rows, 2 * LANES), jnp.float32)],
        name="inverse_rows",
    )(first, second, as_f32(inv * norm), as_f32(inv0 * norm), twist)


def solution(mesh):
    return jax.shard_map(
        on_device,
        mesh=mesh,
        in_specs=(P("map", "rows", None), P(), P(), P(), P()),
        out_specs=P("map", None, "rows", None),
        check_vma=False,
    )
```

```python
import jax
import jax.numpy as jnp
import numpy as np
from jax import lax
from jax.experimental import pallas as pl
from jax.experimental.pallas import tpu as pltpu
from jax.sharding import PartitionSpec as P


LANES = 128


def signed_frequency(positions, length):
    return (
        jnp.where(positions < length // 2, positions, positions - length).astype(jnp.float32)
        / length
    )


def kernel_terms(row_freq, col_freq, total_rows, total_cols):
    wave_rows = signed_frequency(row_freq, total_rows)
    wave_cols = signed_frequency(col_freq, total_cols)
    squared = wave_rows * wave_rows + wave_cols * wave_cols
    denominator = jnp.where(squared > 0, squared, jnp.float32(1.0))
    return (
        (wave_rows * wave_rows - wave_cols * wave_cols) / denominator,
        2.0 * wave_rows * wave_cols / denominator,
    )


def lens_coefficients(lens_weight, bin_distance, plane_bin, source_plane):
    bin_ids = jnp.arange(bin_distance.shape[0], dtype=jnp.int32)
    distance = jnp.sum(
        jnp.where(plane_bin[:, None] == bin_ids[None, :], bin_distance[None, :], jnp.float32(0.0)),
        axis=1,
    )
    planes = jnp.arange(plane_bin.shape[0], dtype=jnp.int32)
    picked = source_plane[:, None] == planes[None, :]
    source_distance = jnp.sum(jnp.where(picked, distance[None, :], jnp.float32(0.0)), axis=1)
    nearer = planes[None, :] <= source_plane[:, None]
    weights = lens_weight[None, :] * (1.0 - distance[None, :] / source_distance[:, None])
    return jnp.where(nearer, weights, jnp.float32(0.0))


def phase_parts(length, left_index, right_index, orient):
    products = left_index[:, None] * right_index[None, :] % length
    angles = 2.0 * jnp.pi / length * products.astype(jnp.float32)
    return (jnp.cos(angles), orient * jnp.sin(angles))


def block_matrix(length, orient, left_index, right_index):
    cos_part, sin_part = phase_parts(length, left_index, right_index, orient)
    return jnp.stack([jnp.stack([cos_part, -sin_part]), jnp.stack([sin_part, cos_part])])


def rotate_phase(values, cos_part, sin_part):
    return jnp.stack(
        [values[0] * cos_part - values[1] * sin_part, values[0] * sin_part + values[1] * cos_part]
    )


def contract(pattern, matrix, values):
    return jnp.einsum(pattern, matrix, values, precision=lax.Precision.HIGHEST)


def general(density, lens_weight, bin_distance, plane_bin, source_plane):
    rows_local = density.shape[1]
    total_cols = density.shape[2]
    devices = lax.axis_size("rows")
    total_rows = rows_local * devices
    col_share = total_cols // devices
    plane_sums = jnp.sum(density, axis=(1, 2), dtype=jnp.float32)
    totals = lax.psum(plane_sums, "rows")
    plane_mean = totals / (total_rows * total_cols)
    coefficients = lens_coefficients(lens_weight, bin_distance, plane_bin, source_plane)
    contrast = density.astype(jnp.float32) / plane_mean[:, None, None] - 1.0
    convergence = jnp.einsum("sl,lxy->sxy", coefficients, contrast, precision=lax.Precision.HIGHEST)
    sources_here = convergence.shape[0]
    across = jnp.arange(devices, dtype=jnp.int32)
    within_rows = jnp.arange(rows_local, dtype=jnp.int32)
    within_cols = jnp.arange(col_share, dtype=jnp.int32)
    first_cos, first_sin = phase_parts(devices, across, across, -1.0)
    first_table = jnp.stack([first_cos, first_sin])
    shaped = convergence.reshape(sources_here, rows_local, devices, col_share)
    partial_value = contract("cka,sxab->csxkb", first_table, shaped)
    twist_cos, twist_sin = phase_parts(total_cols, across, within_cols, -1.0)
    partial_value = rotate_phase(partial_value, twist_cos, twist_sin)
    spectrum_rows = contract(
        "cdjb,dsxkb->csxkj", block_matrix(col_share, -1.0, within_cols, within_cols), partial_value
    )
    forward_devices = block_matrix(devices, -1.0, across, across)
    forward_rows = block_matrix(rows_local, -1.0, within_rows, within_rows)
    inverse_devices = block_matrix(devices, 1.0, across, across)
    inverse_rows = block_matrix(rows_local, 1.0, within_rows, within_rows)
    fwd_cos, fwd_sin = phase_parts(total_rows, within_rows, across, -1.0)
    back_cos, back_sin = phase_parts(total_rows, within_rows, across, 1.0)
    row_freq = (across[None, :] + devices * within_rows[:, None])[:, :, None]
    col_freq = (lax.axis_index("rows") + devices * within_cols)[None, None, :]
    kernel_plus, kernel_cross = kernel_terms(row_freq, col_freq, total_rows, total_cols)
    columns = lax.all_to_all(spectrum_rows, "rows", split_axis=3, concat_axis=3, tiled=True)
    values = contract("cdka,dsxaq->csxkq", forward_devices, columns)
    values = rotate_phase(values, fwd_cos[:, :, None], fwd_sin[:, :, None])
    values = contract("cdjx,dsxkq->csjkq", forward_rows, values)
    sheared = jnp.stack(
        [
            kernel_plus * values[0] - kernel_cross * values[1],
            kernel_plus * values[1] + kernel_cross * values[0],
        ]
    )
    values = contract("cdxj,dsjkq->csxkq", inverse_rows, sheared)
    values = rotate_phase(values, back_cos[:, :, None], back_sin[:, :, None])
    returned = lax.all_to_all(
        contract("cdak,dsxkq->csxaq", inverse_devices, values),
        "rows",
        split_axis=3,
        concat_axis=3,
        tiled=True,
    )
    values = contract(
        "cdbj,dsxkj->csxkb", block_matrix(col_share, 1.0, within_cols, within_cols), returned
    )
    last_cos, last_sin = phase_parts(total_cols, across, within_cols, 1.0)
    values = rotate_phase(values, last_cos, last_sin)
    result = contract("cdak,dsxkb->scxab", inverse_devices, values)
    normalizer = 1.0 / (total_rows * total_cols)
    return result.reshape(sources_here, 2, rows_local, total_cols) * normalizer


def rotate(value, turns, orient):
    re, im = value
    turns = turns % 1.0
    if turns == 0.0:
        return re, im
    cos, sin = float(np.cos(2 * np.pi * turns)), float(orient * np.sin(2 * np.pi * turns))
    if turns == 0.25:
        return (None if im is None else -im * sin if sin != 1.0 else -im), (re if sin > 0 else -re)
    if im is None:
        return re * cos, re * sin
    return re * cos - im * sin, re * sin + im * cos


def plus(a, b):
    return b if a is None else a if b is None else a + b


def minus(a, b):
    return (None if b is None else -b) if a is None else a if b is None else a - b


def real_fft(values):
    n = len(values)
    if n == 1:
        return [(values[0], None)]
    if n == 2:
        return [(values[0] + values[1], None), (values[0] - values[1], None)]
    even, odd = real_fft(values[0::2]), real_fft(values[1::2])
    half, quarter = n // 2, n // 4
    out = [None] * (half + 1)
    for k in range(quarter + 1):
        e, o = even[k], rotate(odd[k], k / n, -1.0)
        out[k] = plus(e[0], o[0]), plus(e[1], o[1])
        if k != half - k:
            diff = minus(e[0], o[0]), minus(e[1], o[1])
            out[half - k] = diff[0], None if diff[1] is None else -diff[1]
    out[0], out[half] = (out[0][0], None), (out[half][0], None)
    return out


def real_inverse(values):
    half = len(values) - 1
    n = 2 * half
    if n == 2:
        return [values[0][0] + values[1][0], values[0][0] - values[1][0]]
    even, odd = [], []
    for k in range(half // 2 + 1):
        a, b = values[k], values[half - k]
        conj_im = None if b[1] is None else -b[1]
        if k == half - k:
            even.append((2.0 * a[0], None))
            odd.append((-2.0 * a[1], None))
            continue
        even.append((a[0] + b[0], plus(a[1], conj_im)))
        odd.append(rotate((a[0] - b[0], minus(a[1], conj_im)), k / n, 1.0))
    even[0], odd[0] = (even[0][0], None), (odd[0][0], None)
    out = [None] * n
    out[0::2], out[1::2] = real_inverse(even), real_inverse(odd)
    return out


def complex_fft(values, orient):
    n = len(values)
    if n == 1:
        return values
    even, odd = complex_fft(values[0::2], orient), complex_fft(values[1::2], orient)
    out = [None] * n
    for k in range(n // 2):
        o = rotate(odd[k], k / n, orient)
        out[k] = even[k][0] + o[0], even[k][1] + o[1]
        out[k + n // 2] = even[k][0] - o[0], even[k][1] - o[1]
    return out


def split(x):
    high = x.astype(jnp.bfloat16)
    return high, (x - high.astype(jnp.float32)).astype(jnp.bfloat16)


def split_dot(left, right, left_dim, right_dim):
    dims = (((left_dim,), (right_dim,)), ((), ()))
    dot = lambda a, b: lax.dot_general(a, b, dims, preferred_element_type=jnp.float32)
    return dot(left[0], right[0]) + (dot(left[0], right[1]) + dot(left[1], right[0]))


def split_table(table):
    high = np.asarray(table, np.float32).astype(jnp.bfloat16)
    return jnp.asarray(np.stack([high, (table - high.astype(np.float64)).astype(jnp.bfloat16)]))


def col_tables(share):
    b = np.arange(LANES)[:, None]
    q = np.arange(LANES)[None, :]
    re_lane = (q // share * 2 * share + q % share)[0]
    im_lane = re_lane + share
    ang = 2 * np.pi * (b * q % LANES) / LANES
    fwd = np.zeros((2 * LANES, 2 * LANES))
    fwd[:LANES, re_lane], fwd[:LANES, im_lane] = np.cos(ang), -np.sin(ang)
    fwd[LANES:, re_lane], fwd[LANES:, im_lane] = np.sin(ang), np.cos(ang)
    inv = fwd.T.copy()
    half = LANES // 2
    fwd0 = np.zeros((2 * LANES, 2 * LANES))
    ang0 = ang[:, :half]
    ang1 = 2 * np.pi * (b * (2 * q[:, :half] + 1) % (2 * LANES)) / (2 * LANES)
    fwd0[:LANES, re_lane[:half]], fwd0[:LANES, im_lane[:half]] = np.cos(ang0), -np.sin(ang0)
    fwd0[LANES:, re_lane[half:]], fwd0[LANES:, im_lane[half:]] = np.cos(ang1), -np.sin(ang1)
    fwd0[:LANES, re_lane[0]], fwd0[:LANES, im_lane[0]] = (-1.0) ** b[:, 0], 1.0
    inv0 = 2.0 * fwd0.T
    inv0[re_lane[0]] *= 0.5
    inv0[im_lane[0]] *= 0.5
    return fwd, fwd0, inv, inv0


def sample_tables(rows):
    r = np.arange(rows)
    ang = 2 * np.pi * (np.outer(r, r) % rows) / rows
    cos, sin = np.cos(ang), np.sin(ang)
    return np.block([[cos, -sin], [sin, cos]]), np.block([[cos, sin], [-sin, cos]])


def twist_table(count, length, total):
    angle = 2 * np.pi * np.outer(np.arange(count), np.arange(length)) / total
    return jnp.asarray(np.stack([np.cos(angle), np.sin(angle)]), jnp.float32)


QUAD = 4
CHUNKS = 2
WAYS = (2, 3, 1)


def swap(values, stride):
    devices = QUAD * QUAD
    out = list(values)
    for g in WAYS:
        out[g] = lax.ppermute(values[g], "rows", [(a, a ^ (stride * g)) for a in range(devices)])
    return out


def regroup(values):
    return [jnp.stack([values[g][i] for g in range(QUAD)]) for i in range(QUAD)]


def exchange(first, second):
    crossed = swap(first, QUAD)
    turned = swap(second, 1)
    last = swap(regroup(turned), QUAD)
    return swap(regroup(crossed), 1), last


def slot(order, plane_bits, inner_bits):
    return (plane_bits, inner_bits) if order == 0 else (inner_bits, plane_bits)


def plane_totals(density_ref, out_ref):
    planes, rows, total_cols = density_ref.shape
    tile = 16
    for l in range(planes):

        def add(t, totals):
            here = pl.ds(pl.multiple_of(t * tile, tile), tile)
            totals = list(totals)
            for a in range(total_cols // LANES):
                totals[a % 4] += density_ref[l, here, a * LANES:(a + 1) * LANES].astype(jnp.float32)
            return tuple(totals)

        zero = jnp.zeros((tile, LANES), jnp.float32)
        t = lax.fori_loop(0, rows // tile, add, (zero,) * 4)
        out_ref[l:l + 1, :] = jnp.sum((t[0] + t[1]) + (t[2] + t[3]), axis=0, keepdims=True)


def transform_rows(chunk, me, held, table_ref, permuted, out_refs):
    plane, inner = me // QUAD, me % QUAD
    part = 2 * LANES // QUAD
    tables = (0, 1) if chunk == 0 else (0,)
    for kind in tables:
        for sp in range(QUAD):
            rows = pl.ds(pl.multiple_of((inner ^ sp) * part, part), part)
            permuted[kind, :, sp * part:(sp + 1) * part, :] = table_ref[kind, :, rows, :]
    for sz in range(QUAD):
        block = plane ^ sz
        kind = jnp.where(block == 0, 1, 0) if chunk == 0 else 0
        table = permuted[kind]
        value = split_dot((table[0], table[1]), split(held[block]), 1, 1)
        for sp in range(QUAD):
            g, i = slot(chunk, sz, sp)
            out_refs[g][i] = value[sp * part:(sp + 1) * part]


def combine_kernel(me_ref, coefficients_ref, *refs):
    totals_refs, (density_ref, table_ref, twist_ref), refs = refs[:QUAD], refs[QUAD:QUAD + 3], refs[QUAD + 3:]
    out_refs, later_ref, held, permuted, scale = refs[:QUAD], refs[QUAD], refs[QUAD + 1], refs[QUAD + 2], refs[QUAD + 3]
    planes, rows, total_cols = density_ref.shape
    groups = total_cols // LANES
    blocks = groups // 2 // CHUNKS
    total = (totals_refs[0][...] + totals_refs[1][...]) + (totals_refs[2][...] + totals_refs[3][...])
    mean = jnp.sum(total, axis=1, keepdims=True) / float(rows * QUAD * QUAD * total_cols)
    coefficients = coefficients_ref[...]
    scale[:planes, :] = coefficients / mean
    scale[planes:planes + 1, :] = jnp.sum(coefficients, axis=0, keepdims=True)
    tile = 16

    def step(t, carry):
        here = pl.ds(pl.multiple_of(t * tile, tile), tile)
        values = []
        for a in range(groups):
            lanes = slice(a * LANES, (a + 1) * LANES)
            value = density_ref[0, here, lanes].astype(jnp.float32) * scale[0:1, :] - scale[planes:planes + 1, :]
            for l in range(1, planes):
                value += density_ref[l, here, lanes].astype(jnp.float32) * scale[l:l + 1, :]
            values.append(value)
        spectrum = real_fft(values)
        held[0, here, :LANES] = spectrum[0][0]
        held[0, here, LANES:] = spectrum[groups // 2][0]
        for k in range(1, groups // 2):
            re, im = spectrum[k]
            cos, sin = twist_ref[0, k:k + 1, :], twist_ref[1, k:k + 1, :]
            target, b = (held, k) if k < blocks else (later_ref, k - blocks)
            target[b, here, :LANES] = re * cos + im * sin
            target[b, here, LANES:] = im * cos - re * sin
        return carry

    lax.fori_loop(0, rows // tile, step, 0)
    transform_rows(0, me_ref[0], held, table_ref, permuted, out_refs)


def later_kernel(me_ref, held, table_ref, *refs):
    transform_rows(1, me_ref[0], held, table_ref, refs[QUAD], refs[:QUAD])


def shear_kernel(chunk, me_ref, *refs):
    in_refs, (fwd_ref, inv_ref, twist_ref) = refs[:QUAD], refs[QUAD:QUAD + 3]
    out_refs = refs[QUAD + 3:2 * QUAD + 3]
    samples, spectra, fields, results, extra = refs[2 * QUAD + 3:]
    devices, part, rows = samples.shape
    share = part // 2
    total_rows, total_cols = devices * rows, 2 * CHUNKS * share * devices
    me = me_ref[0]
    plane, inner = me // QUAD, me % QUAD
    tile = 8
    special = jnp.where(
        (lax.broadcasted_iota(jnp.int32, (part, rows), 0) == share) & (me == 0) & (chunk == 0), 1.0, 0.0
    )
    total = jnp.zeros((part, rows), jnp.float32)
    for sz in range(QUAD):
        for sp in range(QUAD):
            i, g = slot(chunk, sz, sp)
            value = in_refs[g][i]
            if chunk == 0:
                extra[me ^ (QUAD * sz + sp)] = value[share:share + tile]
                total += value
                value = value - special * value
            samples[me ^ (QUAD * sz + sp)] = value

    def forward(t, carry):
        top = pl.ds(pl.multiple_of(t * tile, tile), tile)
        low = pl.ds(pl.multiple_of(share + t * tile, tile), tile)
        out = complex_fft([(samples[a, top, :], samples[a, low, :]) for a in range(devices)], -1.0)
        for k in range(devices):
            re, im = out[k]
            rows_k = pl.ds(pl.multiple_of(k * share + t * tile, tile), tile)
            if k:
                cos, sin = twist_ref[0, k:k + 1, :], twist_ref[1, k:k + 1, :]
                re, im = re * cos + im * sin, im * cos - re * sin
            spectra[rows_k, :rows] = re
            spectra[rows_k, rows:] = im
        return carry

    lax.fori_loop(0, share // tile, forward, 0)

    groups = total_cols // LANES
    block = plane + QUAD * chunk
    q = inner * share + lax.broadcasted_iota(jnp.int32, (share, rows), 0)
    first = jnp.where(q < LANES // 2, groups * q, groups // 2 + groups * (q - LANES // 2))
    first = jnp.where(q == 0, total_cols // 2, first)
    ky = jnp.where(block == 0, first, block + groups * q)
    fy = signed_frequency(ky, total_cols)
    edge_y = jnp.where(ky == total_cols // 2, 1.0, 0.0)
    j = lax.broadcasted_iota(jnp.int32, (share, rows), 1)
    per = LANES // share

    def columns(n, carry):
        here = pl.ds(pl.multiple_of(n * LANES, LANES), LANES)
        value = split_dot(split(spectra[here, :]), (fwd_ref[0], fwd_ref[1]), 1, 0)
        for m in range(per):
            kx = n * per + m + devices * j
            fx = signed_frequency(kx, total_rows)
            squared = fx * fx + fy * fy
            inverse = 1.0 / jnp.where(squared > 0, squared, 1.0)
            even = (fx * fx - fy * fy) * inverse
            cross = 2.0 * fx * fy * inverse
            edge_x = jnp.where(kx == total_rows // 2, 1.0, 0.0)
            odd = cross * (edge_x + edge_y - 2.0 * edge_x * edge_y)
            cross = cross - odd
            re, im = value[m * share:(m + 1) * share, :rows], value[m * share:(m + 1) * share, rows:]
            there = pl.ds(pl.multiple_of(n * LANES + m * share, share), share)
            fields[0, there, :rows] = even * re - odd * im
            fields[0, there, rows:] = even * im + odd * re
            fields[1, there, :rows] = cross * re
            fields[1, there, rows:] = cross * im
        for f in range(2):
            fields[f, here, :] = split_dot(split(fields[f, here, :]), (inv_ref[0], inv_ref[1]), 1, 0)
        return carry

    lax.fori_loop(0, devices // per, columns, 0)

    def backward(t, carry):
        for f in range(2):
            values = []
            for k in range(devices):
                rows_k = pl.ds(pl.multiple_of(k * share + t * tile, tile), tile)
                re, im = fields[f, rows_k, :rows], fields[f, rows_k, rows:]
                if k:
                    cos, sin = twist_ref[0, k:k + 1, :], twist_ref[1, k:k + 1, :]
                    re, im = re * cos - im * sin, re * sin + im * cos
                values.append((re, im))
            out = complex_fft(values, 1.0)
            top = pl.ds(pl.multiple_of(f * part + t * tile, tile), tile)
            low = pl.ds(pl.multiple_of(f * part + share + t * tile, tile), tile)
            for a in range(devices):
                results[a, top, :], results[a, low, :] = out[a]
        return carry

    lax.fori_loop(0, share // tile, backward, 0)
    if chunk == 0:
        mean = jnp.sum(total[share:share + tile], axis=1, keepdims=True) / float(total_rows)
        mask = special[share:share + tile] * float(total_rows)
        for a in range(devices):
            results[a, share:share + tile, :] += (extra[a] - mean) * mask
    for sz in range(QUAD):
        for sp in range(QUAD):
            g, i = slot(1 - chunk, sz, sp)
            out_refs[g][i] = results[me ^ (QUAD * sz + sp)]


def untransform(chunk, me, in_refs, table_ref, twist_ref, columns, held):
    part = columns.shape[2] // QUAD
    for sz in range(QUAD):
        for sp in range(QUAD):
            i, g = slot(1 - chunk, sz, sp)
            source = me ^ (QUAD * sz + sp)
            rows = pl.ds(pl.multiple_of(source % QUAD * part, part), part)
            for f in range(2):
                columns[f, source // QUAD, rows, :] = in_refs[g][i, f * part:(f + 1) * part, :]
    for f in range(2):
        for b in range(QUAD):
            kind = 1 if chunk == 0 and b == 0 else 0
            value = split_dot(split(columns[f, b].T), (table_ref[kind, 0], table_ref[kind, 1]), 1, 0)
            k = chunk * QUAD + b
            if k:
                re, im = value[:, :LANES], value[:, LANES:]
                cos, sin = twist_ref[0, k:k + 1, :], twist_ref[1, k:k + 1, :]
                held[f, b, :, :LANES] = re * cos - im * sin
                held[f, b, :, LANES:] = re * sin + im * cos
            else:
                held[f, b] = value


def early_kernel(me_ref, *refs):
    in_refs, (table_ref, twist_ref, held, columns) = refs[:QUAD], refs[QUAD:]
    untransform(1, me_ref[0], in_refs, table_ref, twist_ref, columns, held)


def final_kernel(me_ref, *refs):
    in_refs, (early_ref, table_ref, twist_ref, out_ref, columns, held) = refs[:QUAD], refs[QUAD:]
    untransform(0, me_ref[0], in_refs, table_ref, twist_ref, columns, held)
    rows, total_cols = out_ref.shape[2:]
    groups = total_cols // LANES
    tile = 8
    for f in range(2):

        def step(t, carry):
            here = pl.ds(pl.multiple_of(t * tile, tile), tile)
            values = [(held[f, 0, here, :LANES], None)]
            for k in range(1, groups // 2):
                source, b = (held, k) if k < QUAD else (early_ref, k - QUAD)
                values.append((source[f, b, here, :LANES], source[f, b, here, LANES:]))
            values.append((held[f, 0, here, LANES:], None))
            out = real_inverse(values)
            for a in range(groups):
                out_ref[0, f, here, a * LANES:(a + 1) * LANES] = out[a]
            return carry

        lax.fori_loop(0, rows // tile, step, 0)


def limit(mebibytes):
    return pltpu.CompilerParams(vmem_limit_bytes=mebibytes << 20)


def smem():
    return pl.BlockSpec(memory_space=pltpu.SMEM)


def vmem():
    return pl.BlockSpec(memory_space=pltpu.VMEM)


def on_device(density, lens_weight, bin_distance, plane_bin, source_plane):
    planes, rows, total_cols = density.shape
    devices = lax.axis_size("rows")
    share = total_cols // 2 // devices // CHUNKS
    part = 2 * share
    groups = total_cols // LANES
    f32 = lambda *shape: jax.ShapeDtypeStruct(shape, jnp.float32)
    me = lax.axis_index("rows").astype(jnp.int32)[None]

    totals = pl.pallas_call(
        plane_totals,
        out_shape=f32(planes, LANES),
        in_specs=[vmem()],
        out_specs=vmem(),
        name="plane_totals",
        compiler_params=limit(4),
    )(density)
    totals = sum(swap([totals] * QUAD, 1))
    totals = swap([totals] * QUAD, QUAD)
    coefficients = lens_coefficients(lens_weight, bin_distance, plane_bin, source_plane)[0]
    coefficients = jnp.broadcast_to(coefficients[:, None], (planes, LANES))

    fwd, fwd0, inv, inv0 = col_tables(share)
    norm = 1.0 / (rows * devices * total_cols)
    fwd_tables = jnp.stack([split_table(fwd.T), split_table(fwd0.T)])
    inv_tables = jnp.stack([split_table(inv * norm), split_table(inv0 * norm)])
    twist = twist_table(groups // 2, LANES, total_cols)
    twist_x = twist_table(devices, rows, devices * rows)
    sample_fwd, sample_inv = (split_table(t) for t in sample_tables(rows))

    quarter = f32(QUAD, part, rows)
    out = pl.pallas_call(
        combine_kernel,
        out_shape=[quarter] * QUAD + [f32(QUAD, rows, 2 * LANES)],
        in_specs=[smem()] + [vmem()] * (QUAD + 4),
        out_specs=[vmem()] * (QUAD + 1),
        scratch_shapes=[
            pltpu.VMEM((QUAD, rows, 2 * LANES), jnp.float32),
            pltpu.VMEM((2, 2, 2 * LANES, 2 * LANES), jnp.bfloat16),
            pltpu.VMEM((planes + 8, LANES), jnp.float32),
        ],
        name="combine",
        compiler_params=limit(12),
    )(me, coefficients, *totals, density, fwd_tables, twist)
    sent = [out[:QUAD]]
    sent.append(
        pl.pallas_call(
            later_kernel,
            out_shape=[quarter] * QUAD,
            in_specs=[smem()] + [vmem()] * 2,
            out_specs=[vmem()] * QUAD,
            scratch_shapes=[pltpu.VMEM((1, 2, 2 * LANES, 2 * LANES), jnp.bfloat16)],
            name="later",
        compiler_params=limit(4),
        )(me, out[QUAD], fwd_tables)
    )
    double = f32(QUAD, 2 * part, rows)
    sheared = []
    for chunk, columns in enumerate(exchange(*sent)):
        sheared.append(
            pl.pallas_call(
                lambda *refs, chunk=chunk: shear_kernel(chunk, *refs),
                out_shape=[double] * QUAD,
                in_specs=[smem()] + [vmem()] * (QUAD + 3),
                out_specs=[vmem()] * QUAD,
                scratch_shapes=[
                    pltpu.VMEM((devices, part, rows), jnp.float32),
                    pltpu.VMEM((devices * share, 2 * rows), jnp.float32),
                    pltpu.VMEM((2, devices * share, 2 * rows), jnp.float32),
                    pltpu.VMEM((devices, 2 * part, rows), jnp.float32),
                    pltpu.VMEM((devices, 8, rows), jnp.float32),
                ],
                compiler_params=limit(10),
            )(me, *columns, sample_fwd, sample_inv, twist_x)
        )
    back = exchange(*sheared[::-1])
    early = pl.pallas_call(
        early_kernel,
        out_shape=f32(2, QUAD, rows, 2 * LANES),
        in_specs=[smem()] + [vmem()] * (QUAD + 2),
        out_specs=vmem(),
        scratch_shapes=[pltpu.VMEM((2, QUAD, 2 * LANES, rows), jnp.float32)],
        name="early",
        compiler_params=limit(8),
    )(me, *back[0], inv_tables, twist)
    return pl.pallas_call(
        final_kernel,
        out_shape=f32(1, 2, rows, total_cols),
        in_specs=[smem()] + [vmem()] * (QUAD + 3),
        out_specs=vmem(),
        scratch_shapes=[
            pltpu.VMEM((2, QUAD, 2 * LANES, rows), jnp.float32),
            pltpu.VMEM((2, QUAD, rows, 2 * LANES), jnp.float32),
        ],
        name="final",
        compiler_params=limit(14),
    )(me, *back[1], early, inv_tables, twist)


def by_shape(density, lens_weight, bin_distance, plane_bin, source_plane):
    rows, total_cols = density.shape[1:]
    devices = lax.axis_size("rows")
    fits = (
        devices == QUAD * QUAD
        and rows == LANES
        and total_cols == 2 * LANES * CHUNKS * QUAD
        and source_plane.shape[0] == 1
    )
    chosen = on_device if fits else general
    return chosen(density, lens_weight, bin_distance, plane_bin, source_plane)


def solution(mesh):
    return jax.shard_map(
        by_shape,
        mesh=mesh,
        in_specs=(P("map", "rows", None), P(), P(), P(), P()),
        out_specs=P("map", None, "rows", None),
        check_vma=False,
    )
```
